32 devices in a mesh: parts: 2 (over y), pol: 4 (over z), scen: 2 (over x), fund: 2 (over core).
Axes of the slice: x: 2, y: 2, z: 4, core: 2. Of those that a mesh axis runs over, the one named last changes fastest.
Arguments:
- count_init: float32 [32768], P(('pol', 'fund')), may hold values from 0.5 to 2
- value_init: float32 [32768], P(('pol', 'fund')), may hold values from 0.5 to 4
- durations: int32 [32768], P(('pol', 'fund')), may hold values from 0 to 119
- products: int32 [32768], P(('pol', 'fund')), may hold values from 0 to 7
- policy_fund: int32 [32768], P(('pol', 'fund')), may hold values from 0 to 119, as said below
- lapse_base: float32 [8], replicated, may hold values from 0.05 to 0.1
- lapse_sens: float32 [8], replicated, may hold values from 6 to 10
- fee_rate: float32 [8], replicated, may hold values from 0.002 to 0.02
- fund_share: float32 [120], replicated, may hold values from 0.3 to 1
- bond_flows: float32 [16384, 120], P(('pol', 'fund')), may hold values from 0.05 to 1
- bond_fund: int32 [16384], P(('pol', 'fund')), may hold values from 0 to 119, as said below
- holdings: float32 [16384], P(('pol', 'fund')), may hold values from 0.037 to 0.3
- scen_rates: float32 [3, 120, 512], P(None, None, ('parts', 'scen')), parts along dimension 2, may hold values from 0 to 0.12
Outputs:
- credited: float32 [3, 120, 512], P(None, None, ('parts', 'scen')), parts along dimension 2
- reserve: float32 [512, 32768], P(('parts', 'scen'), ('pol', 'fund')), parts along dimension 0
The draws below stay inside these ranges and needn't reach their ends.
There are 2 independent parts, one for each index of `parts`. The reference program is written for one: setup_inputs(seed, part) draws one part's arguments, and reference() takes and returns one part's arrays. A program takes and returns all parts, laid end to end along the dimension named above; an argument that names none is the same for every part. Nothing has to cross between parts.
Inputs may be any that keep to these rules, and one draw needn't show every extreme that they name: `policy_fund`: every fund number appears at least once. `bond_fund`: every fund number appears at least once.
All inputs are finite; a program needn't handle non-finite values.
Results may differ from the reference program's by a relative error of at most 0.0003.
Values sent between devices are 32-bit elements; how exact they have to be, the bound alone decides.
A program may use at most 64 MiB of HBM per device.

```python
import math
import jax
import jax.numpy as jnp
from jax import lax

FUNDS = 120
TENORS = 120
PRODUCTS = 8
MONTHS = 3
S_DEV = 128
POLICIES = 32768
BONDS = 16384
SCEN = 256


def covering(key, total_count):
    spread = jax.random.permutation(jax.random.fold_in(key, 17), FUNDS)
    others = jax.random.randint(jax.random.fold_in(key, 29), (total_count,), 0, FUNDS)
    positions = jnp.arange(total_count)
    picked = spread[jnp.minimum(positions, FUNDS - 1)]
    return jnp.where(positions < FUNDS, picked, others).astype(jnp.int32)


def draw_policy_fund(key, part):
    return covering(jax.random.fold_in(key, 5), POLICIES)


def draw_bond_fund(key, part):
    return covering(jax.random.fold_in(key, 7), BONDS)


def with_ends(result, own_key, smallest, top_value):
    extent = result.shape
    place = [jax.random.randint(jax.random.fold_in(own_key, axis), (), 0, extent[axis]) for axis in range(len(extent))]
    result = result.at[tuple(place)].set(smallest)
    longest = extent.index(max(extent))
    place[longest] = (place[longest] + 1) % extent[longest]
    return result.at[tuple(place)].set(top_value)


def levels(key, dims, pieces, smallest, largest):
    loudness, own = 1.0, jax.random.fold_in(key, 6)
    for position, parts in pieces:
        steps = jnp.exp(jax.random.uniform(jax.random.fold_in(own, position), (parts,), jnp.float32, smallest / len(pieces), largest / len(pieces)))
        loudness = loudness * jnp.repeat(steps, dims[position] // parts).reshape([-1 if axis == position else 1 for axis in range(len(dims))])
    return loudness


def setup_inputs(seed: int = 0, part: int = 0) -> dict:
    key_of = jax.random.split(jax.random.key(seed), 14)
    part_keys = jax.random.split(jax.random.fold_in(key_of[13], part), 14)
    count_init = jnp.clip(jnp.exp(math.log(2.0) - 1.3862944 * jax.random.uniform(key_of[0], (POLICIES,), jnp.float32) ** levels(key_of[0], (POLICIES,), ((0, 8),), -0.2, 0.2)), 0.5, 2.0)
    value_init = jnp.clip(jnp.exp(math.log(4.0) - 2.0794415 * jax.random.uniform(key_of[1], (POLICIES,), jnp.float32) ** levels(key_of[1], (POLICIES,), ((0, 8),), -0.2, 0.2)), 0.5, 4.0)
    durations = with_ends(jax.random.randint(key_of[2], (POLICIES,), 0, 120), jax.random.fold_in(key_of[2], 1), 0, 119).astype(jnp.int32)
    products = with_ends(jax.random.randint(key_of[3], (POLICIES,), 0, PRODUCTS), jax.random.fold_in(key_of[3], 1), 0, PRODUCTS - 1).astype(jnp.int32)
    policy_fund = draw_policy_fund(jax.random.fold_in(key_of[13], 71), part)
    lapse_base = jnp.clip(jnp.exp(jax.random.uniform(key_of[5], (PRODUCTS,), jnp.float32, math.log(0.05), math.log(0.1))), 0.05, 0.1)
    lapse_sens = jnp.clip(jax.random.uniform(key_of[6], (PRODUCTS,), jnp.float32, 6.0, 10.0), 6.0, 10.0)
    fee_rate = jnp.clip(jnp.exp(jax.random.uniform(key_of[7], (PRODUCTS,), jnp.float32, math.log(0.002), math.log(0.02))), 0.002, 0.02)
    fund_share = jnp.clip(jnp.exp(jax.random.uniform(key_of[8], (FUNDS,), jnp.float32, math.log(0.3), math.log(1.0))), 0.3, 1.0)
    bond_flows = jnp.clip(jnp.exp(math.log(1.0) - 2.9957323 * jax.random.uniform(key_of[9], (BONDS, TENORS), jnp.float32) ** levels(key_of[9], (BONDS, TENORS), ((0, 8),), -0.2, 0.2)), 0.05, 1.0)
    bond_fund = draw_bond_fund(jax.random.fold_in(key_of[13], 71), part)
    holdings = jnp.clip(jnp.exp(math.log(0.3) - 2.0928646 * jax.random.uniform(key_of[11], (BONDS,), jnp.float32) ** levels(key_of[11], (BONDS,), ((0, 8),), -0.2, 0.2)), 0.037, 0.3)
    scen_rates = jnp.clip(0.12 * jax.random.uniform(part_keys[12], (MONTHS, TENORS, SCEN), jnp.float32) ** levels(part_keys[12], (MONTHS, TENORS, SCEN), ((2, 2),), -0.2, 0.2), 0.0, 0.12)
    return dict(count_init=count_init, value_init=value_init, durations=durations, products=products, policy_fund=policy_fund, lapse_base=lapse_base, lapse_sens=lapse_sens, fee_rate=fee_rate, fund_share=fund_share, bond_flows=bond_flows, bond_fund=bond_fund, holdings=holdings, scen_rates=scen_rates)


surrender_end = 84
highest = lax.Precision.HIGHEST


def project_block(block_rates, count_init, value_init, durations, products, policy_fund, lapse_base, lapse_sens, fee_rate, fund_share, bond_flows, bond_fund, holdings):
    tenor_years = (jnp.arange(TENORS).astype(jnp.float32) + 1.0) / 12.0
    width_scen = block_rates.shape[2]
    lapse_pol = lapse_base[products]
    sens_pol = lapse_sens[products]
    fee_pol = fee_rate[products]
    in_force = jnp.broadcast_to(count_init[None, :], (width_scen, POLICIES))
    account = jnp.broadcast_to(value_init[None, :], (width_scen, POLICIES))
    credited_list = []
    for month_idx in range(MONTHS):
        discount = jnp.exp(-block_rates[month_idx] * tenor_years[:, None])
        bond_values = jnp.dot(bond_flows, discount, precision=highest, preferred_element_type=jnp.float32)
        assets = jax.ops.segment_sum(bond_values * holdings[:, None], bond_fund, num_segments=FUNDS)
        reserve = in_force * account
        liabilities = jax.ops.segment_sum(reserve.T, policy_fund, num_segments=FUNDS)
        credited = fund_share[:, None] * jnp.log(assets / liabilities)
        credit_pol = credited[policy_fund].T
        market = block_rates[month_idx, TENORS - 1]
        later_mult = jnp.where(durations + month_idx >= surrender_end, 2.0, 1.0)
        lapse_now = (lapse_pol * later_mult)[None, :] * jnp.exp(sens_pol[None, :] * (market[:, None] - credit_pol))
        in_force = in_force * jnp.exp(-lapse_now)
        account = account * jnp.exp(credit_pol / 12.0 - fee_pol[None, :])
        credited_list.append(credited)
    return jnp.stack(credited_list), in_force * account


def reference(count_init, value_init, durations, products, policy_fund, lapse_base, lapse_sens, fee_rate, fund_share, bond_flows, bond_fund, holdings, scen_rates):
    block_count = SCEN // S_DEV
    blocked = scen_rates.reshape(MONTHS, TENORS, block_count, S_DEV).transpose(2, 0, 1, 3)

    def one_block(block_rates):
        return project_block(block_rates, count_init, value_init, durations, products, policy_fund, lapse_base, lapse_sens, fee_rate, fund_share, bond_flows, bond_fund, holdings)

    credited_blocks, reserve_blocks = lax.map(one_block, blocked)
    credited = credited_blocks.transpose(1, 2, 0, 3).reshape(MONTHS, FUNDS, SCEN)
    reserve = reserve_blocks.reshape(SCEN, POLICIES)
    return (credited, reserve)
```

```python
import functools

import jax
import jax.numpy as jnp
from jax import lax
from jax.experimental import pallas as pl
from jax.experimental.pallas import tpu as pltpu
from jax.sharding import PartitionSpec as P

surrender_end = 84
lanes = 128
f32, bf16 = jnp.float32, jnp.bfloat16
contract_cols = (((1,), (1,)), ((), ()))


def round_up(value, unit):
    return -(-value // unit) * unit


def split(value):
    high = value.astype(bf16)
    return high, (value - high.astype(f32)).astype(bf16)


def dot(left, right):
    return jnp.dot(left, right, preferred_element_type=f32)


def dot_cols(left, right):
    return lax.dot_general(left, right, contract_cols, preferred_element_type=f32)


def onehot(ids_row, row_count):
    rows = lax.broadcasted_iota(jnp.int32, (row_count, ids_row.shape[1]), 0)
    return rows == ids_row


def gather_kernel(
    group,
    months,
    kinds,
    funds,
    count_ref,
    value_ref,
    dur_ref,
    prod_ref,
    pfund_ref,
    flows_ref,
    bfund_ref,
    hold_ref,
    out_ref,
    part_buf,
    recv_buf,
    sum_buf,
    send_a,
    recv_a,
    send_b,
    recv_b,
):
    pol_devs, fund_devs = group
    n = pol_devs * fund_devs
    me = lax.axis_index("pol") * fund_devs + lax.axis_index("fund")

    def peer_of(step):
        peer = lax.rem(me + step, n)
        return peer, {"pol": peer // fund_devs, "fund": lax.rem(peer, fund_devs)}

    barrier = pltpu.get_barrier_semaphore()
    for step in range(1, n):
        pl.semaphore_signal(
            barrier, inc=1, device_id=peer_of(step)[1], device_id_type=pl.DeviceIdType.MESH
        )

    wide = part_buf.shape[2]
    chunk = part_buf.shape[1]
    part_buf[...] = jnp.zeros_like(part_buf)

    held = jnp.where(onehot(bfund_ref[...], funds), hold_ref[...], 0.0)
    held_h, held_l = split(held)
    flow_h, flow_l = split(flows_ref[...])
    weights = dot_cols(held_h, flow_h) + (
        dot_cols(held_h, flow_l) + dot_cols(held_l, flow_h)
    )

    worth = count_ref[...] * value_ref[...]
    late = jnp.clip(dur_ref[...] - (surrender_end - (months - 1)), 0, months - 1)
    kind = late * kinds + prod_ref[...]
    classed = jnp.where(onehot(kind, months * kinds), worth, 0.0)
    pol_hot = onehot(pfund_ref[...], wide).astype(f32).astype(bf16)
    worth_h, worth_l = split(classed)
    classes = dot_cols(worth_h, pol_hot) + dot_cols(worth_l, pol_hot)

    def put(values, first):
        row = first
        while row < first + values.shape[0]:
            slot, inner = row // chunk, row % chunk
            size = min(chunk - inner, first + values.shape[0] - row)
            part_buf[slot, inner : inner + size, : values.shape[1]] = values[
                row - first : row - first + size
            ]
            row += size

    put(weights, 0)
    put(classes, funds)

    pl.semaphore_wait(barrier, n - 1)

    def scatter(step):
        peer, where = peer_of(step)
        return pltpu.make_async_remote_copy(
            src_ref=part_buf.at[peer],
            dst_ref=recv_buf.at[me],
            send_sem=send_a.at[peer],
            recv_sem=recv_a.at[me],
            device_id=where,
            device_id_type=pl.DeviceIdType.MESH,
        )

    def spread(step):
        peer, where = peer_of(step)
        return pltpu.make_async_remote_copy(
            src_ref=sum_buf.at[me],
            dst_ref=sum_buf.at[me],
            send_sem=send_b.at[peer],
            recv_sem=recv_b.at[me],
            device_id=where,
            device_id_type=pl.DeviceIdType.MESH,
        )

    def arrival(buf, sems, step):
        peer, where = peer_of(step)
        return pltpu.make_async_remote_copy(
            src_ref=buf.at[peer],
            dst_ref=buf.at[peer],
            send_sem=send_a.at[peer],
            recv_sem=sems.at[peer],
            device_id=where,
            device_id_type=pl.DeviceIdType.MESH,
        )

    for step in range(1, n):
        scatter(step).start()
    total = part_buf[me]
    for step in range(1, n):
        arrival(recv_buf, recv_a, step).wait_recv()
        total = total + recv_buf[peer_of(step)[0]]
    sum_buf[me] = total
    for step in range(1, n):
        spread(step).start()
    for step in range(1, n):
        arrival(sum_buf, recv_b, step).wait_recv()
    for slot in range(n):
        out_ref[slot * chunk : (slot + 1) * chunk, :] = sum_buf[slot]
    for step in range(1, n):
        scatter(step).wait_send()
        spread(step).wait_send()


def project_kernel(
    months,
    kinds,
    funds,
    block,
    base_ref,
    sens_ref,
    fee_ref,
    share_ref,
    sums_ref,
    rates_ref,
    count_ref,
    value_ref,
    dur_ref,
    prod_ref,
    pfund_ref,
    cred_ref,
    out_ref,
    table,
    gathered,
    rows,
    market_sum,
    staged,
    out_sems,
):
    tenors = rates_ref.shape[1]
    scen = rates_ref.shape[2]
    wide = sums_ref.shape[1]
    policies = count_ref.shape[1]

    products = prod_ref[...]
    base = jnp.zeros(products.shape, f32)
    sens = base
    fee = base
    for k in range(kinds):
        match = products == k
        base = jnp.where(match, base_ref[k], base)
        sens = jnp.where(match, sens_ref[k], sens)
        fee = jnp.where(match, fee_ref[k], fee)
    rows[0:1, :] = count_ref[...] * value_ref[...]
    rows[1:2, :] = sens
    rows[2:3, :] = -float(months) * fee
    for t in range(months):
        rows[3 + t : 4 + t, :] = -jnp.where(dur_ref[...] + t >= surrender_end, 2.0, 1.0) * base

    tenor_years = (
        lax.broadcasted_iota(jnp.int32, (1, tenors), 1).astype(f32) + 1.0
    ) / 12.0
    weights = sums_ref[0:funds, 0:tenors]
    weight_h, weight_l = split(weights)
    start = [
        [sums_ref[funds + u * kinds + k : funds + u * kinds + k + 1, :] for k in range(kinds)]
        for u in range(months)
    ]
    exp_fee = [jnp.exp(jnp.full((1, wide), -fee_ref[k], f32)) for k in range(kinds)]
    lane = lax.broadcasted_iota(jnp.int32, (scen, wide), 1)
    share = share_ref[...]
    if wide > funds:
        share = jnp.concatenate([share, jnp.zeros((1, wide - funds), f32)], axis=1)
    factors = None
    growth = None
    for t in range(months):
        rates = rates_ref[t].T
        disc_h, disc_l = split(jnp.exp(-rates * tenor_years))
        assets = dot_cols(disc_h, weight_h) + (
            dot_cols(disc_h, weight_l) + dot_cols(disc_l, weight_h)
        )
        if wide > funds:
            assets = jnp.concatenate([assets, jnp.ones((scen, wide - funds), f32)], axis=1)
        if factors is None:
            liab = functools.reduce(jnp.add, [w for line in start for w in line])
        else:
            parts = [
                start[u][k] * factors[u][k] for u in range(months) for k in range(kinds)
            ]
            liab = functools.reduce(jnp.add, parts) * jnp.exp(growth)
        credited = jnp.where(lane < funds, share * jnp.log(assets / liab), 0.0)
        cred_ref[t] = credited.T[:funds]
        market = rates[:, tenors - 1 : tenors]
        spread = market - credited
        table[t * scen : (t + 1) * scen, 0:wide] = spread.astype(bf16)
        table[t * scen : (t + 1) * scen, wide : 2 * wide] = split(spread)[1]
        market_all = market if t == 0 else market_all + market
        growth = credited / 12.0 if t == 0 else growth + credited / 12.0
        if t < months - 1:
            stay = [jnp.exp(-base_ref[k] * jnp.exp(sens_ref[k] * spread)) for k in range(kinds)]
            new = []
            for u in range(months):
                line = []
                for k in range(kinds):
                    step = stay[k] * stay[k] if u >= months - 1 - t else stay[k]
                    line.append(step if factors is None else factors[u][k] * step)
                new.append(line)
            factors = new
            start = [[start[u][k] * exp_fee[k] for k in range(kinds)] for u in range(months)]
    market_sum[...] = jnp.broadcast_to(market_all / 12.0, (scen, lanes))

    tile = min(scen, 32)

    def out_copy(idx):
        cols = pl.ds(pl.multiple_of(idx * block, block), block)
        return pltpu.make_async_copy(staged.at[idx], out_ref.at[:, cols], out_sems.at[idx])

    @pl.loop(0, policies // block)
    def _(idx):
        cols = pl.ds(pl.multiple_of(idx * block, block), block)
        hot = jnp.where(onehot(pfund_ref[:, cols], wide), 1.0, 0.0).astype(bf16)
        gathered[...] = dot(table[...], jnp.concatenate([hot, hot], axis=0))
        worth = rows[0:1, cols]
        sens_row = rows[1:2, cols]
        fee_row = rows[2:3, cols]
        for first in range(0, scen, tile):
            acc = fee_row + jnp.tile(market_sum[first : first + tile, :], (1, block // lanes))
            spread_sum = None
            for t in range(months):
                spread = gathered[t * scen + first : t * scen + first + tile, :]
                acc = acc + rows[3 + t : 4 + t, cols] * jnp.exp(sens_row * spread)
                spread_sum = spread if t == 0 else spread_sum + spread
            staged[idx, first : first + tile, :] = worth * jnp.exp(
                acc - spread_sum * (1.0 / 12.0)
            )
        out_copy(idx).start()

    @pl.loop(0, policies // block)
    def _(idx):
        out_copy(idx).wait()


def local(
    group,
    count_init,
    value_init,
    durations,
    products,
    policy_fund,
    lapse_base,
    lapse_sens,
    fee_rate,
    fund_share,
    bond_flows,
    bond_fund,
    holdings,
    scen_rates,
):
    funds = fund_share.shape[0]
    months, tenors, scen = scen_rates.shape
    kinds = lapse_base.shape[0]
    policies = count_init.shape[0]
    n = group[0] * group[1]
    wide = round_up(max(funds, tenors), lanes)
    chunk = -(-(funds + months * kinds) // n)
    vmem = pl.BlockSpec(memory_space=pltpu.VMEM)
    smem = pl.BlockSpec(memory_space=pltpu.SMEM)
    count_row, value_row, dur_row, prod_row, pfund_row, bfund_row, hold_row = (
        x[None, :]
        for x in (
            count_init,
            value_init,
            durations,
            products,
            policy_fund,
            bond_fund,
            holdings,
        )
    )
    sums = pl.pallas_call(
        functools.partial(gather_kernel, group, months, kinds, funds),
        out_shape=jax.ShapeDtypeStruct((n * chunk, wide), f32),
        in_specs=[vmem] * 8,
        out_specs=vmem,
        scratch_shapes=[
            pltpu.VMEM((n, chunk, wide), f32),
            pltpu.VMEM((n, chunk, wide), f32),
            pltpu.VMEM((n, chunk, wide), f32),
            pltpu.SemaphoreType.DMA((n,)),
            pltpu.SemaphoreType.DMA((n,)),
            pltpu.SemaphoreType.DMA((n,)),
            pltpu.SemaphoreType.DMA((n,)),
        ],
        compiler_params=pltpu.CompilerParams(collective_id=0, has_side_effects=True),
        name="fund_sums",
    )(
        count_row,
        value_row,
        dur_row,
        prod_row,
        pfund_row,
        bond_flows.T,
        bfund_row,
        hold_row,
    )
    block = 256 if policies % 256 == 0 else policies
    return pl.pallas_call(
        functools.partial(project_kernel, months, kinds, funds, block),
        out_shape=(
            jax.ShapeDtypeStruct((months, funds, scen), f32),
            jax.ShapeDtypeStruct((scen, policies), f32),
        ),
        in_specs=[smem] * 3 + [vmem] * 8,
        out_specs=(vmem, pl.BlockSpec(memory_space=pl.ANY)),
        scratch_shapes=[
            pltpu.VMEM((months * scen, 2 * wide), bf16),
            pltpu.VMEM((months * scen, block), f32),
            pltpu.VMEM((round_up(3 + months, 8), policies), f32),
            pltpu.VMEM((scen, lanes), f32),
            pltpu.VMEM((policies // block, scen, block), f32),
            pltpu.SemaphoreType.DMA((policies // block,)),
        ],
        name="project",
    )(
        lapse_base,
        lapse_sens,
        fee_rate,
        fund_share[None, :],
        sums,
        scen_rates,
        count_row,
        value_row,
        dur_row,
        prod_row,
        pfund_row,
    )


def solution(mesh):
    in_specs = (
        P(("pol", "fund")),
        P(("pol", "fund")),
        P(("pol", "fund")),
        P(("pol", "fund")),
        P(("pol", "fund")),
        P(),
        P(),
        P(),
        P(),
        P(("pol", "fund"), None),
        P(("pol", "fund")),
        P(("pol", "fund")),
        P(None, None, ("parts", "scen")),
    )
    out_specs = (P(None, None, ("parts", "scen")), P(("parts", "scen"), ("pol", "fund")))
    group = (mesh.shape["pol"], mesh.shape["fund"])
    return jax.shard_map(
        functools.partial(local, group),
        mesh=mesh,
        in_specs=in_specs,
        out_specs=out_specs,
        check_vma=False,
    )
```

```python
import functools

import jax
import jax.numpy as jnp
from jax import lax
from jax.experimental import pallas as pl
from jax.experimental.pallas import tpu as pltpu
from jax.sharding import PartitionSpec as P

surrender_end = 84
lanes = 128
log2_e = 1.4426950408889634
f32, bf16 = jnp.float32, jnp.bfloat16
contract_cols = (((1,), (1,)), ((), ()))


def round_up(value, unit):
    return -(-value // unit) * unit


def split(value):
    high = value.astype(bf16)
    return high, (value - high.astype(f32)).astype(bf16)


def dot(left, right):
    return jnp.dot(left, right, preferred_element_type=f32)


def dot_cols(left, right):
    return lax.dot_general(left, right, contract_cols, preferred_element_type=f32)


def onehot(ids_row, values, row_count):
    shape = (16, ids_row.shape[1])
    kind = bf16 if row_count <= 256 else f32
    ids = jnp.broadcast_to(ids_row.astype(f32), shape).astype(kind)
    rows = lax.broadcasted_iota(jnp.int32, shape, 0).astype(f32)
    values = [jnp.broadcast_to(v, shape).astype(bf16) for v in values]
    masks = [ids == (rows + float(g)).astype(kind) for g in range(0, row_count, 16)]
    zero = jnp.zeros(shape, bf16)
    return [jnp.concatenate([jnp.where(m, v, zero) for m in masks], axis=0) for v in values]


def split_row(row):
    high = row.astype(bf16).astype(f32)
    return high, row - high


def gather_kernel(
    group,
    kinds,
    funds,
    bfund_hbm,
    hold_hbm,
    flows_hbm,
    pfund_hbm,
    count_hbm,
    value_hbm,
    dur_hbm,
    prod_hbm,
    base_hbm,
    sens_hbm,
    fee_hbm,
    share_hbm,
    rates_hbm,
    out_ref,
    hot_ref,
    rows_ref,
    disc_ref,
    market_ref,
    kind_ref,
    share_ref,
    bfund_ref,
    hold_ref,
    flows_ref,
    pfund_ref,
    count_ref,
    value_ref,
    dur_ref,
    prod_ref,
    base_ref,
    sens_ref,
    fee_ref,
    rates_ref,
    in_sems,
    part_buf,
    recv_buf,
    sum_buf,
    send_a,
    recv_a,
    send_b,
    recv_b,
):
    pol_devs, fund_devs = group
    n = pol_devs * fund_devs
    pairs = (
        (bfund_hbm, bfund_ref),
        (hold_hbm, hold_ref),
        (flows_hbm, flows_ref),
        (pfund_hbm, pfund_ref),
        (count_hbm, count_ref),
        (value_hbm, value_ref),
        (dur_hbm, dur_ref),
        (prod_hbm, prod_ref),
        (base_hbm, base_ref),
        (sens_hbm, sens_ref),
        (fee_hbm, fee_ref),
        (share_hbm, share_ref),
        (rates_hbm, rates_ref),
    )
    loads = [
        pltpu.make_async_copy(src, dst, in_sems.at[i]) for i, (src, dst) in enumerate(pairs)
    ]
    for load in loads:
        load.start()
    me = lax.axis_index("pol") * fund_devs + lax.axis_index("fund")

    def peer_of(step):
        peer = lax.rem(me + step, n)
        return peer, {"pol": peer // fund_devs, "fund": lax.rem(peer, fund_devs)}

    barrier = pltpu.get_barrier_semaphore()
    for step in range(1, n):
        pl.semaphore_signal(
            barrier, inc=1, device_id=peer_of(step)[1], device_id_type=pl.DeviceIdType.MESH
        )

    months, tenors, scen = rates_ref.shape
    wide = part_buf.shape[2]
    chunk = part_buf.shape[1]
    part_buf[...] = jnp.zeros_like(part_buf)

    for load in loads[:3]:
        load.wait()
    flows = flows_ref[...]
    if wide > tenors:
        flows = jnp.concatenate(
            [flows, jnp.zeros((wide - tenors, flows.shape[1]), f32)], axis=0
        )
    held = jnp.concatenate(onehot(bfund_ref[...], split_row(hold_ref[...]), wide), axis=0)
    quads = dot_cols(held, jnp.concatenate(split(flows), axis=0))
    weights = (quads[:funds, :wide] + quads[wide : wide + funds, wide:]) + (
        quads[:funds, wide:] + quads[wide : wide + funds, :wide]
    )

    for load in loads[3:8]:
        load.wait()
    worth = count_ref[...] * value_ref[...]
    late = jnp.clip(dur_ref[...] - (surrender_end - (months - 1)), 0, months - 1)
    kind = late * kinds + prod_ref[...]
    classed = onehot(kind, split_row(worth), round_up(months * kinds, 16))
    (pol_hot,) = onehot(pfund_ref[...], [jnp.ones(worth.shape, f32)], wide)
    hot_ref[...] = pol_hot
    sides = dot_cols(jnp.concatenate(classed, axis=0), pol_hot)
    half = sides.shape[0] // 2
    classes = (sides[:half] + sides[half:])[: months * kinds]

    def put(values, first):
        row = first
        while row < first + values.shape[0]:
            slot, inner = row // chunk, row % chunk
            size = min(chunk - inner, first + values.shape[0] - row)
            part_buf[slot, inner : inner + size, : values.shape[1]] = values[
                row - first : row - first + size
            ]
            row += size

    put(weights, 0)
    put(classes, funds)

    pl.semaphore_wait(barrier, n - 1)

    def scatter(step):
        peer, where = peer_of(step)
        return pltpu.make_async_remote_copy(
            src_ref=part_buf.at[peer],
            dst_ref=recv_buf.at[me],
            send_sem=send_a.at[peer],
            recv_sem=recv_a.at[me],
            device_id=where,
            device_id_type=pl.DeviceIdType.MESH,
        )

    def spread(step):
        peer, where = peer_of(step)
        return pltpu.make_async_remote_copy(
            src_ref=sum_buf.at[me],
            dst_ref=sum_buf.at[me],
            send_sem=send_b.at[peer],
            recv_sem=recv_b.at[me],
            device_id=where,
            device_id_type=pl.DeviceIdType.MESH,
        )

    def arrival(buf, sems, step):
        peer, where = peer_of(step)
        return pltpu.make_async_remote_copy(
            src_ref=buf.at[peer],
            dst_ref=buf.at[peer],
            send_sem=send_a.at[peer],
            recv_sem=sems.at[peer],
            device_id=where,
            device_id_type=pl.DeviceIdType.MESH,
        )

    for step in range(1, n):
        scatter(step).start()

    for load in loads[8:]:
        load.wait()
    for k in range(kinds):
        kind_ref[k : k + 1, :] = jnp.full((1, wide), -log2_e * base_ref[k], f32)
        kind_ref[kinds + k : kinds + k + 1, :] = jnp.full((1, wide), 12.0 * sens_ref[k], f32)
        kind_ref[2 * kinds + k : 2 * kinds + k + 1, :] = jnp.exp(
            jnp.full((1, wide), -fee_ref[k], f32)
        )
    products = prod_ref[...]
    base = jnp.zeros(products.shape, f32)
    sens = base
    fee = base
    for k in range(kinds):
        match = products == k
        base = jnp.where(match, base_ref[k], base)
        sens = jnp.where(match, sens_ref[k], sens)
        fee = jnp.where(match, fee_ref[k], fee)
    rows_ref[0:1, :] = jnp.log2(worth) - (months * log2_e) * fee
    rows_ref[1:2, :] = 12.0 * sens
    for t in range(months):
        rows_ref[2 + t : 3 + t, :] = base * jnp.where(
            dur_ref[...] + t >= surrender_end, -2.0 * log2_e, -log2_e
        )

    total = part_buf[me]
    for step in range(1, n):
        arrival(recv_buf, recv_a, step).wait_recv()
        total = total + recv_buf[peer_of(step)[0]]
    sum_buf[me] = total
    for step in range(1, n):
        spread(step).start()

    tenor_years = (
        lax.broadcasted_iota(jnp.int32, (1, tenors), 1).astype(f32) + 1.0
    ) / 12.0
    disc_ref[...] = jnp.zeros_like(disc_ref)
    for t in range(months):
        rates = rates_ref[t].T
        disc_h, disc_l = split(jnp.exp(-rates * tenor_years))
        span = slice(t * scen, (t + 1) * scen)
        disc_ref[span, 0:tenors] = disc_h
        disc_ref[span, wide : wide + tenors] = disc_l
        market_ref[span, :] = jnp.broadcast_to(rates[:, tenors - 1 : tenors], (scen, wide))

    for step in range(1, n):
        arrival(sum_buf, recv_b, step).wait_recv()
    for slot in range(n):
        out_ref[slot * chunk : (slot + 1) * chunk, :] = sum_buf[slot]
    for step in range(1, n):
        scatter(step).wait_send()
        spread(step).wait_send()


def project_kernel(
    kinds,
    funds,
    block,
    sums_ref,
    hot_ref,
    rows,
    disc_ref,
    market_ref,
    kind_ref,
    share_ref,
    cred_ref,
    out_ref,
    table,
    assets_buf,
    gathered,
    market_sum,
    staged,
    out_sems,
):
    months = cred_ref.shape[0]
    scen = cred_ref.shape[2]
    wide = sums_ref.shape[1]
    policies = hot_ref.shape[1]

    weights = sums_ref[0:funds, :]
    if wide > funds:
        weights = jnp.concatenate([weights, jnp.zeros((wide - funds, wide), f32)], axis=0)
    weight_h, weight_l = split(weights)
    both = jnp.concatenate(
        [
            jnp.concatenate([weight_h, weight_h], axis=1),
            jnp.concatenate([weight_l, weight_l], axis=1),
        ],
        axis=0,
    )
    halves = dot_cols(disc_ref[...], both)
    assets_buf[...] = halves[:, :wide] + halves[:, wide:]

    base_rows, sens_rows, exp_fee = (
        [kind_ref[i * kinds + k : i * kinds + k + 1, :] for k in range(kinds)] for i in range(3)
    )
    start = [
        [[sums_ref[funds + u * kinds + k : funds + u * kinds + k + 1, :] for k in range(kinds)]
         for u in range(months)]
    ]
    for t in range(1, months):
        start.append([[w * e for w, e in zip(line, exp_fee)] for line in start[-1]])
    share = share_ref[...]
    if wide > funds:
        share = jnp.concatenate([share, jnp.zeros((1, wide - funds), f32)], axis=1)

    tile = min(scen, 32)
    lane = lax.broadcasted_iota(jnp.int32, (tile, wide), 1)
    for first in range(0, scen, tile):
        stays = []
        growth = None
        market_all = None
        for t in range(months):
            span = slice(t * scen + first, t * scen + first + tile)
            liab = None
            for k in range(kinds):
                acc = start[t][months - 1][k]
                for u in range(months - 1, 0, -1):
                    early = months - 1 - u
                    if early < t:
                        acc = acc * stays[early][k]
                    acc = acc + start[t][u - 1][k]
                for early in range(t):
                    acc = acc * stays[early][k]
                liab = acc if liab is None else liab + acc
            if growth is not None:
                liab = liab * jnp.exp2(growth)
            ratio = jnp.where(lane < funds, assets_buf[span, :] / liab, 1.0)
            credited = share * jnp.log(ratio)
            cred_ref[t, :, first : first + tile] = credited.T[:funds]
            market = market_ref[span, :]
            scaled = (market - credited) * (log2_e / 12.0)
            high, low = split(scaled)
            table[span, 0:wide] = high
            table[span, wide : 2 * wide] = low
            moved = credited * (log2_e / 12.0)
            growth = moved if growth is None else growth + moved
            market_all = market if market_all is None else market_all + market
            if t < months - 1:
                stays.append(
                    [
                        jnp.exp2(base_rows[k] * jnp.exp2(sens_rows[k] * scaled))
                        for k in range(kinds)
                    ]
                )
        market_sum[first : first + tile, :] = market_all[:, :lanes] * (log2_e / 12.0)

    def out_copy(idx):
        cols = pl.ds(pl.multiple_of(idx * block, block), block)
        return pltpu.make_async_copy(staged.at[idx], out_ref.at[:, cols], out_sems.at[idx])

    def fetch(idx, slot):
        cols = pl.ds(pl.multiple_of(idx * block, block), block)
        hot = hot_ref[:, cols]
        gathered[slot] = dot(table[...], jnp.concatenate([hot, hot], axis=0))

    def settle(idx, slot):
        cols = pl.ds(pl.multiple_of(idx * block, block), block)
        first_row = rows[0:1, cols]
        sens_row = rows[1:2, cols]
        for first in range(0, scen, tile):
            acc = first_row + jnp.tile(market_sum[first : first + tile, :], (1, block // lanes))
            for t in range(months):
                spread = gathered[slot, t * scen + first : t * scen + first + tile, :]
                acc = acc + (rows[2 + t : 3 + t, cols] * jnp.exp2(sens_row * spread) - spread)
            staged[idx, first : first + tile, :] = jnp.exp2(acc)
        out_copy(idx).start()

    blocks = policies // block
    fetch(0, 0)

    @pl.loop(0, blocks, step=2)
    def _(idx):
        fetch(idx + 1, 1)
        settle(idx, 0)
        fetch(jnp.minimum(idx + 2, blocks - 1), 0)
        settle(idx + 1, 1)

    @pl.loop(0, blocks)
    def _(idx):
        out_copy(idx).wait()


def local(
    group,
    count_init,
    value_init,
    durations,
    products,
    policy_fund,
    lapse_base,
    lapse_sens,
    fee_rate,
    fund_share,
    bond_flows,
    bond_fund,
    holdings,
    scen_rates,
):
    funds = fund_share.shape[0]
    months, tenors, scen = scen_rates.shape
    kinds = lapse_base.shape[0]
    policies = count_init.shape[0]
    n = group[0] * group[1]
    wide = round_up(max(funds, tenors), lanes)
    chunk = -(-(funds + months * kinds) // n)
    vmem = pl.BlockSpec(memory_space=pltpu.VMEM)
    count_row, value_row, dur_row, prod_row, pfund_row, bfund_row, hold_row = (
        x[None, :]
        for x in (
            count_init,
            value_init,
            durations,
            products,
            policy_fund,
            bond_fund,
            holdings,
        )
    )
    few = 24 << 20
    hbm = pl.BlockSpec(memory_space=pltpu.HBM)
    sources = (
        bfund_row,
        hold_row,
        bond_flows.T,
        pfund_row,
        count_row,
        value_row,
        dur_row,
        prod_row,
        lapse_base,
        lapse_sens,
        fee_rate,
        fund_share[None, :],
        scen_rates,
    )
    carried = pl.pallas_call(
        functools.partial(gather_kernel, group, kinds, funds),
        out_shape=(
            jax.ShapeDtypeStruct((n * chunk, wide), f32),
            jax.ShapeDtypeStruct((wide, policies), bf16),
            jax.ShapeDtypeStruct((round_up(2 + months, 8), policies), f32),
            jax.ShapeDtypeStruct((months * scen, 2 * wide), bf16),
            jax.ShapeDtypeStruct((months * scen, wide), f32),
            jax.ShapeDtypeStruct((3 * kinds, wide), f32),
            jax.ShapeDtypeStruct((1, funds), f32),
        ),
        in_specs=[hbm] * len(sources),
        out_specs=(vmem,) * 7,
        scratch_shapes=[
            *(pltpu.VMEM(x.shape, x.dtype) for x in sources[:8]),
            *(pltpu.SMEM(x.shape, x.dtype) for x in sources[8:11]),
            pltpu.VMEM(scen_rates.shape, f32),
            pltpu.SemaphoreType.DMA((len(sources),)),
            pltpu.VMEM((n, chunk, wide), f32),
            pltpu.VMEM((n, chunk, wide), f32),
            pltpu.VMEM((n, chunk, wide), f32),
            pltpu.SemaphoreType.DMA((n,)),
            pltpu.SemaphoreType.DMA((n,)),
            pltpu.SemaphoreType.DMA((n,)),
            pltpu.SemaphoreType.DMA((n,)),
        ],
        compiler_params=pltpu.CompilerParams(
            collective_id=0, has_side_effects=True, vmem_limit_bytes=few
        ),
        name="fund_sums",
    )(*(pltpu.with_memory_space_constraint(x, pltpu.HBM) for x in sources))
    block = policies // (2 * max(1, policies // 512))
    return pl.pallas_call(
        functools.partial(project_kernel, kinds, funds, block),
        out_shape=(
            jax.ShapeDtypeStruct((months, funds, scen), f32),
            jax.ShapeDtypeStruct((scen, policies), f32),
        ),
        in_specs=[vmem] * 7,
        out_specs=(vmem, pl.BlockSpec(memory_space=pl.ANY)),
        scratch_shapes=[
            pltpu.VMEM((months * scen, 2 * wide), bf16),
            pltpu.VMEM((months * scen, wide), f32),
            pltpu.VMEM((2, months * scen, block), f32),
            pltpu.VMEM((scen, lanes), f32),
            pltpu.VMEM((policies // block, scen, block), f32),
            pltpu.SemaphoreType.DMA((policies // block,)),
        ],
        compiler_params=pltpu.CompilerParams(vmem_limit_bytes=few),
        name="project",
    )(*carried)


def solution(mesh):
    in_specs = (
        P(("pol", "fund")),
        P(("pol", "fund")),
        P(("pol", "fund")),
        P(("pol", "fund")),
        P(("pol", "fund")),
        P(),
        P(),
        P(),
        P(),
        P(("pol", "fund"), None),
        P(("pol", "fund")),
        P(("pol", "fund")),
        P(None, None, ("parts", "scen")),
    )
    out_specs = (P(None, None, ("parts", "scen")), P(("parts", "scen"), ("pol", "fund")))
    group = (mesh.shape["pol"], mesh.shape["fund"])
    return jax.shard_map(
        functools.partial(local, group),
        mesh=mesh,
        in_specs=in_specs,
        out_specs=out_specs,
        check_vma=False,
    )
```

```python
import functools

import jax
import jax.numpy as jnp
from jax import lax
from jax.experimental import pallas as pl
from jax.experimental.pallas import tpu as pltpu
from jax.sharding import PartitionSpec as P

surrender_end = 84
lanes = 128
log2_e = 1.4426950408889634
f32, bf16 = jnp.float32, jnp.bfloat16
contract_cols = (((1,), (1,)), ((), ()))


def round_up(value, unit):
    return -(-value // unit) * unit


def split(value):
    high = value.astype(bf16)
    return high, (value - high.astype(f32)).astype(bf16)


def dot(left, right):
    return jnp.dot(left, right, preferred_element_type=f32)


def dot_cols(left, right):
    return lax.dot_general(left, right, contract_cols, preferred_element_type=f32)


def onehot(ids_row, values, row_count):
    shape = (16, ids_row.shape[1])
    kind = bf16 if row_count <= 256 else f32
    ids = jnp.broadcast_to(ids_row.astype(f32), shape).astype(kind)
    rows = lax.broadcasted_iota(jnp.int32, shape, 0).astype(f32)
    values = [jnp.broadcast_to(v, shape).astype(bf16) for v in values]
    masks = [ids == (rows + float(g)).astype(kind) for g in range(0, row_count, 16)]
    zero = jnp.zeros(shape, bf16)
    return [jnp.concatenate([jnp.where(m, v, zero) for m in masks], axis=0) for v in values]


def split_row(row):
    high = row.astype(bf16).astype(f32)
    return high, row - high


def gather_kernel(
    group,
    kinds,
    funds,
    bfund_hbm,
    hold_hbm,
    flows_hbm,
    pfund_hbm,
    count_hbm,
    value_hbm,
    dur_hbm,
    prod_hbm,
    base_hbm,
    sens_hbm,
    fee_hbm,
    share_hbm,
    rates_hbm,
    out_ref,
    hot_ref,
    rows_ref,
    disc_ref,
    market_ref,
    kind_ref,
    share_ref,
    bfund_ref,
    hold_ref,
    flows_ref,
    pfund_ref,
    count_ref,
    value_ref,
    dur_ref,
    prod_ref,
    base_ref,
    sens_ref,
    fee_ref,
    rates_ref,
    in_sems,
    part_buf,
    recv_buf,
    sum_buf,
    send_a,
    recv_a,
    send_b,
    recv_b,
):
    pol_devs, fund_devs = group
    n = pol_devs * fund_devs
    pairs = (
        (bfund_hbm, bfund_ref),
        (hold_hbm, hold_ref),
        (flows_hbm, flows_ref),
        (pfund_hbm, pfund_ref),
        (count_hbm, count_ref),
        (value_hbm, value_ref),
        (dur_hbm, dur_ref),
        (prod_hbm, prod_ref),
        (base_hbm, base_ref),
        (sens_hbm, sens_ref),
        (fee_hbm, fee_ref),
        (share_hbm, share_ref),
        (rates_hbm, rates_ref),
    )
    loads = [
        pltpu.make_async_copy(src, dst, in_sems.at[i]) for i, (src, dst) in enumerate(pairs)
    ]
    for load in loads:
        load.start()
    me = lax.axis_index("pol") * fund_devs + lax.axis_index("fund")

    def peer_of(step):
        peer = lax.rem(me + step, n)
        return peer, {"pol": peer // fund_devs, "fund": lax.rem(peer, fund_devs)}

    barrier = pltpu.get_barrier_semaphore()
    for step in range(1, n):
        pl.semaphore_signal(
            barrier, inc=1, device_id=peer_of(step)[1], device_id_type=pl.DeviceIdType.MESH
        )

    months, tenors, scen = rates_ref.shape
    wide = part_buf.shape[2]
    chunk = part_buf.shape[1]
    part_buf[...] = jnp.zeros_like(part_buf)

    for load in loads[3:8]:
        load.wait()
    worth = count_ref[...] * value_ref[...]
    late = jnp.clip(dur_ref[...] - (surrender_end - (months - 1)), 0, months - 1)
    kind = late * kinds + prod_ref[...]
    classed = onehot(kind, split_row(worth), round_up(months * kinds, 16))
    (pol_hot,) = onehot(pfund_ref[...], [jnp.ones(worth.shape, f32)], wide)
    hot_ref[...] = pol_hot
    sides = dot_cols(jnp.concatenate(classed, axis=0), pol_hot)
    half = sides.shape[0] // 2
    classes = (sides[:half] + sides[half:])[: months * kinds]

    for load in loads[:3]:
        load.wait()
    flows = flows_ref[...]
    if wide > tenors:
        flows = jnp.concatenate(
            [flows, jnp.zeros((wide - tenors, flows.shape[1]), f32)], axis=0
        )
    held = jnp.concatenate(onehot(bfund_ref[...], split_row(hold_ref[...]), wide), axis=0)
    quads = dot_cols(held, jnp.concatenate(split(flows), axis=0))
    weights = (quads[:funds, :wide] + quads[wide : wide + funds, wide:]) + (
        quads[:funds, wide:] + quads[wide : wide + funds, :wide]
    )

    def put(values, first):
        row = first
        while row < first + values.shape[0]:
            slot, inner = row // chunk, row % chunk
            size = min(chunk - inner, first + values.shape[0] - row)
            part_buf[slot, inner : inner + size, : values.shape[1]] = values[
                row - first : row - first + size
            ]
            row += size

    put(weights, 0)
    put(classes, funds)

    pl.semaphore_wait(barrier, n - 1)

    def scatter(step):
        peer, where = peer_of(step)
        return pltpu.make_async_remote_copy(
            src_ref=part_buf.at[peer],
            dst_ref=recv_buf.at[me],
            send_sem=send_a.at[peer],
            recv_sem=recv_a.at[me],
            device_id=where,
            device_id_type=pl.DeviceIdType.MESH,
        )

    def spread(step):
        peer, where = peer_of(step)
        return pltpu.make_async_remote_copy(
            src_ref=sum_buf.at[me],
            dst_ref=sum_buf.at[me],
            send_sem=send_b.at[peer],
            recv_sem=recv_b.at[me],
            device_id=where,
            device_id_type=pl.DeviceIdType.MESH,
        )

    def arrival(buf, sems, step):
        peer, where = peer_of(step)
        return pltpu.make_async_remote_copy(
            src_ref=buf.at[peer],
            dst_ref=buf.at[peer],
            send_sem=send_a.at[peer],
            recv_sem=sems.at[peer],
            device_id=where,
            device_id_type=pl.DeviceIdType.MESH,
        )

    for step in range(1, n):
        scatter(step).start()

    for load in loads[8:]:
        load.wait()
    for k in range(kinds):
        kind_ref[k : k + 1, :] = jnp.full((1, wide), -log2_e * base_ref[k], f32)
        kind_ref[kinds + k : kinds + k + 1, :] = jnp.full((1, wide), 12.0 * sens_ref[k], f32)
        kind_ref[2 * kinds + k : 2 * kinds + k + 1, :] = jnp.exp(
            jnp.full((1, wide), -fee_ref[k], f32)
        )
    products = prod_ref[...]
    base = jnp.zeros(products.shape, f32)
    sens = base
    fee = base
    for k in range(kinds):
        match = products == k
        base = jnp.where(match, base_ref[k], base)
        sens = jnp.where(match, sens_ref[k], sens)
        fee = jnp.where(match, fee_ref[k], fee)
    rows_ref[0:1, :] = jnp.log2(worth) - (months * log2_e) * fee
    rows_ref[1:2, :] = 12.0 * sens
    for t in range(months):
        rows_ref[2 + t : 3 + t, :] = base * jnp.where(
            dur_ref[...] + t >= surrender_end, -2.0 * log2_e, -log2_e
        )

    total = part_buf[me]
    for step in range(1, n):
        arrival(recv_buf, recv_a, step).wait_recv()
        total = total + recv_buf[peer_of(step)[0]]
    sum_buf[me] = total
    for step in range(1, n):
        spread(step).start()

    tenor_years = (
        lax.broadcasted_iota(jnp.int32, (1, tenors), 1).astype(f32) + 1.0
    ) / 12.0
    disc_ref[...] = jnp.zeros_like(disc_ref)
    for t in range(months):
        rates = rates_ref[t].T
        disc_h, disc_l = split(jnp.exp(-rates * tenor_years))
        span = slice(t * scen, (t + 1) * scen)
        disc_ref[span, 0:tenors] = disc_h
        disc_ref[span, wide : wide + tenors] = disc_l
        market_ref[span, :] = jnp.broadcast_to(rates[:, tenors - 1 : tenors], (scen, wide))

    for step in range(1, n):
        arrival(sum_buf, recv_b, step).wait_recv()
    for slot in range(n):
        out_ref[slot * chunk : (slot + 1) * chunk, :] = sum_buf[slot]
    for step in range(1, n):
        scatter(step).wait_send()
        spread(step).wait_send()


def project_kernel(
    kinds,
    funds,
    block,
    sums_ref,
    hot_ref,
    rows,
    disc_ref,
    market_ref,
    kind_ref,
    share_ref,
    cred_ref,
    out_ref,
    table,
    assets_buf,
    credited_buf,
    gathered_even,
    gathered_odd,
    market_sum,
    staged,
    out_sems,
):
    months = cred_ref.shape[0]
    scen = cred_ref.shape[2]
    wide = sums_ref.shape[1]
    policies = hot_ref.shape[1]

    weights = sums_ref[0:funds, :]
    if wide > funds:
        weights = jnp.concatenate([weights, jnp.zeros((wide - funds, wide), f32)], axis=0)
    weight_h, weight_l = split(weights)
    both = jnp.concatenate(
        [
            jnp.concatenate([weight_h, weight_h], axis=1),
            jnp.concatenate([weight_l, weight_l], axis=1),
        ],
        axis=0,
    )
    halves = dot_cols(disc_ref[...], both)
    assets_buf[...] = halves[:, :wide] + halves[:, wide:]

    base_rows, sens_rows, exp_fee = (
        [kind_ref[i * kinds + k : i * kinds + k + 1, :] for k in range(kinds)] for i in range(3)
    )
    start = [
        [[sums_ref[funds + u * kinds + k : funds + u * kinds + k + 1, :] for k in range(kinds)]
         for u in range(months)]
    ]
    for t in range(1, months):
        start.append([[w * e for w, e in zip(line, exp_fee)] for line in start[-1]])
    share = share_ref[...]
    if wide > funds:
        share = jnp.concatenate([share, jnp.zeros((1, wide - funds), f32)], axis=1)

    tile = min(scen, 32)
    lane = lax.broadcasted_iota(jnp.int32, (tile, wide), 1)
    for first in range(0, scen, tile):
        stays = []
        growth = None
        market_all = None
        for t in range(months):
            span = slice(t * scen + first, t * scen + first + tile)
            liab = None
            for k in range(kinds):
                acc = start[t][months - 1][k]
                for u in range(months - 1, 0, -1):
                    early = months - 1 - u
                    if early < t:
                        acc = acc * stays[early][k]
                    acc = acc + start[t][u - 1][k]
                for early in range(t):
                    acc = acc * stays[early][k]
                liab = acc if liab is None else liab + acc
            if growth is not None:
                liab = liab * jnp.exp2(growth)
            ratio = jnp.where(lane < funds, assets_buf[span, :] / liab, 1.0)
            credited = share * jnp.log(ratio)
            credited_buf[span, :] = credited
            market = market_ref[span, :]
            scaled = (market - credited) * (log2_e / 12.0)
            high, low = split(scaled)
            table[span, 0:wide] = high
            table[span, wide : 2 * wide] = low
            moved = credited * (log2_e / 12.0)
            growth = moved if growth is None else growth + moved
            market_all = market if market_all is None else market_all + market
            if t < months - 1:
                stays.append(
                    [
                        jnp.exp2(base_rows[k] * jnp.exp2(sens_rows[k] * scaled))
                        for k in range(kinds)
                    ]
                )
        market_sum[first : first + tile, :] = market_all[:, :lanes] * (log2_e / 12.0)

    def out_copy(idx):
        cols = pl.ds(pl.multiple_of(idx * block, block), block)
        return pltpu.make_async_copy(staged.at[idx], out_ref.at[:, cols], out_sems.at[idx])

    def fetch(idx, gathered):
        cols = pl.ds(pl.multiple_of(idx * block, block), block)
        hot = hot_ref[:, cols]
        gathered[...] = dot(table[...], jnp.concatenate([hot, hot], axis=0))

    def settle(idx, gathered):
        cols = pl.ds(pl.multiple_of(idx * block, block), block)
        first_row = rows[0:1, cols]
        sens_row = rows[1:2, cols]
        for first in range(0, scen, tile):
            acc = first_row + jnp.tile(market_sum[first : first + tile, :], (1, block // lanes))
            for t in range(months):
                spread = gathered[t * scen + first : t * scen + first + tile, :]
                acc = acc + (rows[2 + t : 3 + t, cols] * jnp.exp2(sens_row * spread) - spread)
            staged[idx, first : first + tile, :] = jnp.exp2(acc)
        out_copy(idx).start()

    def turn(t):
        span = pl.ds(pl.multiple_of(t * scen, scen), scen)
        cred_ref[t] = credited_buf[span, :].T[:funds]

    blocks = policies // block
    fetch(0, gathered_even)
    inside = blocks // 2 >= months
    if not inside:
        for t in range(months):
            turn(t)

    @pl.loop(0, blocks // 2)
    def _(pair):
        idx = 2 * pair
        fetch(idx + 1, gathered_odd)
        settle(idx, gathered_even)
        fetch(jnp.minimum(idx + 2, blocks - 1), gathered_even)
        settle(idx + 1, gathered_odd)
        if inside:
            turn(jnp.minimum(pair, months - 1))

    @pl.loop(0, blocks)
    def _(idx):
        out_copy(idx).wait()


def local(
    group,
    count_init,
    value_init,
    durations,
    products,
    policy_fund,
    lapse_base,
    lapse_sens,
    fee_rate,
    fund_share,
    bond_flows,
    bond_fund,
    holdings,
    scen_rates,
):
    funds = fund_share.shape[0]
    months, tenors, scen = scen_rates.shape
    kinds = lapse_base.shape[0]
    policies = count_init.shape[0]
    n = group[0] * group[1]
    wide = round_up(max(funds, tenors), lanes)
    chunk = -(-(funds + months * kinds) // n)
    vmem = pl.BlockSpec(memory_space=pltpu.VMEM)
    count_row, value_row, dur_row, prod_row, pfund_row, bfund_row, hold_row = (
        x[None, :]
        for x in (
            count_init,
            value_init,
            durations,
            products,
            policy_fund,
            bond_fund,
            holdings,
        )
    )
    few = 24 << 20
    hbm = pl.BlockSpec(memory_space=pltpu.HBM)
    sources = (
        bfund_row,
        hold_row,
        bond_flows.T,
        pfund_row,
        count_row,
        value_row,
        dur_row,
        prod_row,
        lapse_base,
        lapse_sens,
        fee_rate,
        fund_share[None, :],
        scen_rates,
    )
    carried = pl.pallas_call(
        functools.partial(gather_kernel, group, kinds, funds),
        out_shape=(
            jax.ShapeDtypeStruct((n * chunk, wide), f32),
            jax.ShapeDtypeStruct((wide, policies), bf16),
            jax.ShapeDtypeStruct((round_up(2 + months, 8), policies), f32),
            jax.ShapeDtypeStruct((months * scen, 2 * wide), bf16),
            jax.ShapeDtypeStruct((months * scen, wide), f32),
            jax.ShapeDtypeStruct((3 * kinds, wide), f32),
            jax.ShapeDtypeStruct((1, funds), f32),
        ),
        in_specs=[hbm] * len(sources),
        out_specs=(vmem,) * 7,
        scratch_shapes=[
            *(pltpu.VMEM(x.shape, x.dtype) for x in sources[:8]),
            *(pltpu.SMEM(x.shape, x.dtype) for x in sources[8:11]),
            pltpu.VMEM(scen_rates.shape, f32),
            pltpu.SemaphoreType.DMA((len(sources),)),
            pltpu.VMEM((n, chunk, wide), f32),
            pltpu.VMEM((n, chunk, wide), f32),
            pltpu.VMEM((n, chunk, wide), f32),
            pltpu.SemaphoreType.DMA((n,)),
            pltpu.SemaphoreType.DMA((n,)),
            pltpu.SemaphoreType.DMA((n,)),
            pltpu.SemaphoreType.DMA((n,)),
        ],
        compiler_params=pltpu.CompilerParams(
            collective_id=0, has_side_effects=True, vmem_limit_bytes=few
        ),
        name="fund_sums",
    )(*(pltpu.with_memory_space_constraint(x, pltpu.HBM) for x in sources))
    block = policies // (2 * max(1, policies // 512))
    return pl.pallas_call(
        functools.partial(project_kernel, kinds, funds, block),
        out_shape=(
            jax.ShapeDtypeStruct((months, funds, scen), f32),
            jax.ShapeDtypeStruct((scen, policies), f32),
        ),
        in_specs=[vmem] * 7,
        out_specs=(vmem, pl.BlockSpec(memory_space=pl.ANY)),
        scratch_shapes=[
            pltpu.VMEM((months * scen, 2 * wide), bf16),
            pltpu.VMEM((months * scen, wide), f32),
            pltpu.VMEM((months * scen, wide), f32),
            pltpu.VMEM((months * scen, block), f32),
            pltpu.VMEM((months * scen, block), f32),
            pltpu.VMEM((scen, lanes), f32),
            pltpu.VMEM((policies // block, scen, block), f32),
            pltpu.SemaphoreType.DMA((policies // block,)),
        ],
        compiler_params=pltpu.CompilerParams(vmem_limit_bytes=few),
        name="project",
    )(*carried)


def solution(mesh):
    in_specs = (
        P(("pol", "fund")),
        P(("pol", "fund")),
        P(("pol", "fund")),
        P(("pol", "fund")),
        P(("pol", "fund")),
        P(),
        P(),
        P(),
        P(),
        P(("pol", "fund"), None),
        P(("pol", "fund")),
        P(("pol", "fund")),
        P(None, None, ("parts", "scen")),
    )
    out_specs = (P(None, None, ("parts", "scen")), P(("parts", "scen"), ("pol", "fund")))
    group = (mesh.shape["pol"], mesh.shape["fund"])
    return jax.shard_map(
        functools.partial(local, group),
        mesh=mesh,
        in_specs=in_specs,
        out_specs=out_specs,
        check_vma=False,
    )
```

```python
import functools

import jax
import jax.numpy as jnp
from jax import lax
from jax.experimental import pallas as pl
from jax.experimental.pallas import tpu as pltpu
from jax.sharding import PartitionSpec as P

surrender_end = 84
lanes = 128
log2_e = 1.4426950408889634
f32, bf16 = jnp.float32, jnp.bfloat16
contract_cols = (((1,), (1,)), ((), ()))


def round_up(value, unit):
    return -(-value // unit) * unit


def split(value):
    high = value.astype(bf16)
    return high, (value - high.astype(f32)).astype(bf16)


def dot(left, right):
    return jnp.dot(left, right, preferred_element_type=f32)


def dot_cols(left, right):
    return lax.dot_general(left, right, contract_cols, preferred_element_type=f32)


def onehot(ids_row, values, row_count, id_limit):
    shape = (16, ids_row.shape[1])
    kind = bf16 if max(row_count, id_limit) <= 256 else f32
    ids = jnp.broadcast_to(ids_row.astype(f32), shape).astype(kind)
    rows = lax.broadcasted_iota(jnp.int32, shape, 0).astype(f32)
    values = [jnp.broadcast_to(v, shape).astype(bf16) for v in values]
    masks = [ids == (rows + float(g)).astype(kind) for g in range(0, row_count, 16)]
    zero = jnp.zeros(shape, bf16)
    return [jnp.concatenate([jnp.where(m, v, zero) for m in masks], axis=0) for v in values]


def split_row(row):
    high = row.astype(bf16).astype(f32)
    return high, row - high


def gather_kernel(
    group,
    kinds,
    funds,
    bfund_hbm,
    hold_hbm,
    flows_hbm,
    pfund_hbm,
    count_hbm,
    value_hbm,
    dur_hbm,
    prod_hbm,
    base_hbm,
    sens_hbm,
    fee_hbm,
    share_hbm,
    rates_hbm,
    out_ref,
    hot_ref,
    rows_ref,
    disc_ref,
    market_ref,
    kind_ref,
    share_ref,
    bfund_ref,
    hold_ref,
    flows_ref,
    pfund_ref,
    count_ref,
    value_ref,
    dur_ref,
    prod_ref,
    base_ref,
    sens_ref,
    fee_ref,
    rates_ref,
    in_sems,
    part_buf,
    core_buf,
    recv_buf,
    sum_buf,
    core_sems,
    pol_sems,
    slot_sems,
):
    pol_devs, scen_devs, fund_devs = group
    at_pol, at_scen, at_fund = (lax.axis_index(name) for name in ("pol", "scen", "fund"))
    slots = scen_devs * fund_devs
    slot = at_scen * fund_devs + at_fund
    pairs = (
        (bfund_hbm, bfund_ref),
        (hold_hbm, hold_ref),
        (flows_hbm, flows_ref),
        (pfund_hbm, pfund_ref),
        (count_hbm, count_ref),
        (value_hbm, value_ref),
        (dur_hbm, dur_ref),
        (prod_hbm, prod_ref),
        (base_hbm, base_ref),
        (sens_hbm, sens_ref),
        (fee_hbm, fee_ref),
        (share_hbm, share_ref),
        (rates_hbm, rates_ref),
    )
    loads = [
        pltpu.make_async_copy(src, dst, in_sems.at[i]) for i, (src, dst) in enumerate(pairs)
    ]
    for load in loads:
        load.start()

    def pol_peer(step):
        peer = lax.rem(at_pol + step, pol_devs)
        return peer, {"pol": peer}

    def fund_peer(step):
        peer = lax.rem(at_fund + step, fund_devs)
        return peer, {"fund": peer}

    def slot_peer(step):
        peer = lax.rem(slot + step, slots)
        return peer, {"scen": peer // fund_devs, "fund": lax.rem(peer, fund_devs)}

    barrier = pltpu.get_barrier_semaphore()
    greeted = [pol_peer(step)[1] for step in range(1, pol_devs)]
    greeted += [slot_peer(step)[1] for step in range(1, slots)]
    for where in greeted:
        pl.semaphore_signal(
            barrier, inc=1, device_id=where, device_id_type=pl.DeviceIdType.MESH
        )

    months, tenors, scen = rates_ref.shape
    wide = part_buf.shape[2]
    chunk = part_buf.shape[1]
    part_buf[...] = jnp.zeros_like(part_buf)
    fund_rows = -(-funds // scen_devs)
    class_rows = -(-(months * kinds) // scen_devs)

    for load in loads[3:8]:
        load.wait()
    worth = count_ref[...] * value_ref[...]
    late = jnp.clip(dur_ref[...] - (surrender_end - (months - 1)), 0, months - 1)
    kind = late * kinds + prod_ref[...]
    classed = onehot(
        kind - at_scen * class_rows, split_row(worth), round_up(class_rows, 16), months * kinds
    )
    (pol_hot,) = onehot(pfund_ref[...], [jnp.ones(worth.shape, f32)], wide, funds)
    hot_ref[...] = pol_hot
    sides = dot_cols(jnp.concatenate(classed, axis=0), pol_hot)
    half = sides.shape[0] // 2
    classes = (sides[:half] + sides[half:])[:class_rows]

    for load in loads[:3]:
        load.wait()
    flows = flows_ref[...]
    if wide > tenors:
        flows = jnp.concatenate(
            [flows, jnp.zeros((wide - tenors, flows.shape[1]), f32)], axis=0
        )
    held_rows = round_up(fund_rows, 16)
    held = onehot(
        bfund_ref[...] - at_scen * fund_rows, split_row(hold_ref[...]), held_rows, funds
    )
    held = jnp.concatenate(held, axis=0)
    quads = dot_cols(held, jnp.concatenate(split(flows), axis=0))
    upper, lower = quads[:fund_rows], quads[held_rows : held_rows + fund_rows]
    weights = (upper[:, :wide] + lower[:, wide:]) + (upper[:, wide:] + lower[:, :wide])

    def put(values, first):
        row = first
        while row < first + values.shape[0]:
            core, inner = row // chunk, row % chunk
            size = min(chunk - inner, first + values.shape[0] - row)
            part_buf[core, inner : inner + size, : values.shape[1]] = values[
                row - first : row - first + size
            ]
            row += size

    put(weights, 0)
    put(classes, fund_rows)

    pl.semaphore_wait(barrier, len(greeted))

    def send(src, dst, sems, mine, to):
        peer, where = to
        return pltpu.make_async_remote_copy(
            src_ref=src,
            dst_ref=dst,
            send_sem=sems.at[0, peer],
            recv_sem=sems.at[1, mine],
            device_id=where,
            device_id_type=pl.DeviceIdType.MESH,
        )

    def arrive(buf, sems, to):
        peer = to[0]
        send(buf.at[peer], buf.at[peer], sems, peer, to).wait_recv()

    swaps = [
        send(part_buf.at[fund_peer(i)[0]], core_buf.at[at_fund], core_sems, at_fund, fund_peer(i))
        for i in range(1, fund_devs)
    ]
    for copy in swaps:
        copy.start()
    half_sum = part_buf[at_fund]
    for i in range(1, fund_devs):
        arrive(core_buf, core_sems, fund_peer(i))
        half_sum = half_sum + core_buf[fund_peer(i)[0]]
    recv_buf[at_pol] = half_sum

    parts = [
        send(recv_buf.at[at_pol], recv_buf.at[at_pol], pol_sems, at_pol, pol_peer(i))
        for i in range(1, pol_devs)
    ]
    for copy in parts:
        copy.start()

    for load in loads[8:]:
        load.wait()
    for k in range(kinds):
        kind_ref[k : k + 1, :] = jnp.full((1, wide), -log2_e * base_ref[k], f32)
        kind_ref[kinds + k : kinds + k + 1, :] = jnp.full((1, wide), 12.0 * sens_ref[k], f32)
        kind_ref[2 * kinds + k : 2 * kinds + k + 1, :] = jnp.exp(
            jnp.full((1, wide), -fee_ref[k], f32)
        )
    products = prod_ref[...]
    base = jnp.zeros(products.shape, f32)
    sens = base
    fee = base
    for k in range(kinds):
        match = products == k
        base = jnp.where(match, base_ref[k], base)
        sens = jnp.where(match, sens_ref[k], sens)
        fee = jnp.where(match, fee_ref[k], fee)
    rows_ref[0:1, :] = jnp.log2(worth) - (months * log2_e) * fee
    rows_ref[1:2, :] = 12.0 * sens
    for t in range(months):
        rows_ref[2 + t : 3 + t, :] = base * jnp.where(
            dur_ref[...] + t >= surrender_end, -2.0 * log2_e, -log2_e
        )

    for i in range(1, pol_devs):
        arrive(recv_buf, pol_sems, pol_peer(i))
    total = recv_buf[0]
    for i in range(1, pol_devs):
        total = total + recv_buf[i]
    sum_buf[slot] = total

    wholes = [
        send(sum_buf.at[slot], sum_buf.at[slot], slot_sems, slot, slot_peer(i))
        for i in range(1, slots)
    ]
    for copy in wholes:
        copy.start()

    tenor_years = (
        lax.broadcasted_iota(jnp.int32, (1, tenors), 1).astype(f32) + 1.0
    ) / 12.0
    disc_ref[...] = jnp.zeros_like(disc_ref)
    for t in range(months):
        rates = rates_ref[t].T
        disc_h, disc_l = split(jnp.exp(-rates * tenor_years))
        span = slice(t * scen, (t + 1) * scen)
        disc_ref[span, 0:tenors] = disc_h
        disc_ref[span, wide : wide + tenors] = disc_l
        market_ref[span, :] = jnp.broadcast_to(rates[:, tenors - 1 : tenors], (scen, wide))

    for i in range(1, slots):
        arrive(sum_buf, slot_sems, slot_peer(i))
    for column in range(scen_devs):
        block = jnp.concatenate(
            [sum_buf[column * fund_devs + core] for core in range(fund_devs)], axis=0
        )
        out_ref[column * fund_rows : (column + 1) * fund_rows, :] = block[:fund_rows]
        first = scen_devs * fund_rows + column * class_rows
        out_ref[first : first + class_rows, :] = block[fund_rows : fund_rows + class_rows]
    for copy in swaps + parts + wholes:
        copy.wait_send()


def project_kernel(
    class_at,
    kinds,
    funds,
    block,
    sums_ref,
    hot_ref,
    rows,
    disc_ref,
    market_ref,
    kind_ref,
    share_ref,
    cred_ref,
    out_ref,
    table,
    assets_buf,
    credited_buf,
    gathered_even,
    gathered_odd,
    market_sum,
    staged,
    out_sems,
):
    months = cred_ref.shape[0]
    scen = cred_ref.shape[2]
    wide = sums_ref.shape[1]
    policies = hot_ref.shape[1]

    weights = sums_ref[0:funds, :]
    if wide > funds:
        weights = jnp.concatenate([weights, jnp.zeros((wide - funds, wide), f32)], axis=0)
    weight_h, weight_l = split(weights)
    both = jnp.concatenate(
        [
            jnp.concatenate([weight_h, weight_h], axis=1),
            jnp.concatenate([weight_l, weight_l], axis=1),
        ],
        axis=0,
    )
    halves = dot_cols(disc_ref[...], both)
    assets_buf[...] = halves[:, :wide] + halves[:, wide:]

    base_rows, sens_rows, exp_fee = (
        [kind_ref[i * kinds + k : i * kinds + k + 1, :] for k in range(kinds)] for i in range(3)
    )
    start = [
        [[sums_ref[class_at + u * kinds + k : class_at + u * kinds + k + 1, :] for k in range(kinds)]
         for u in range(months)]
    ]
    for t in range(1, months):
        start.append([[w * e for w, e in zip(line, exp_fee)] for line in start[-1]])
    share = share_ref[...]
    if wide > funds:
        share = jnp.concatenate([share, jnp.zeros((1, wide - funds), f32)], axis=1)

    tile = min(scen, 32)
    lane = lax.broadcasted_iota(jnp.int32, (tile, wide), 1)
    for first in range(0, scen, tile):
        stays = []
        growth = None
        market_all = None
        for t in range(months):
            span = slice(t * scen + first, t * scen + first + tile)
            liab = None
            for k in range(kinds):
                acc = start[t][months - 1][k]
                for u in range(months - 1, 0, -1):
                    early = months - 1 - u
                    if early < t:
                        acc = acc * stays[early][k]
                    acc = acc + start[t][u - 1][k]
                for early in range(t):
                    acc = acc * stays[early][k]
                liab = acc if liab is None else liab + acc
            if growth is not None:
                liab = liab * jnp.exp2(growth)
            ratio = jnp.where(lane < funds, assets_buf[span, :] / liab, 1.0)
            credited = share * jnp.log(ratio)
            credited_buf[span, :] = credited
            market = market_ref[span, :]
            scaled = (market - credited) * (log2_e / 12.0)
            high, low = split(scaled)
            table[span, 0:wide] = high
            table[span, wide : 2 * wide] = low
            moved = credited * (log2_e / 12.0)
            growth = moved if growth is None else growth + moved
            market_all = market if market_all is None else market_all + market
            if t < months - 1:
                stays.append(
                    [
                        jnp.exp2(base_rows[k] * jnp.exp2(sens_rows[k] * scaled))
                        for k in range(kinds)
                    ]
                )
        market_sum[first : first + tile, :] = market_all[:, :lanes] * (log2_e / 12.0)

    def out_copy(idx):
        cols = pl.ds(pl.multiple_of(idx * block, block), block)
        return pltpu.make_async_copy(staged.at[idx], out_ref.at[:, cols], out_sems.at[idx])

    def fetch(idx, gathered):
        cols = pl.ds(pl.multiple_of(idx * block, block), block)
        hot = hot_ref[:, cols]
        gathered[...] = dot(table[...], jnp.concatenate([hot, hot], axis=0))

    def settle(idx, gathered):
        cols = pl.ds(pl.multiple_of(idx * block, block), block)
        first_row = rows[0:1, cols]
        sens_row = rows[1:2, cols]
        for first in range(0, scen, tile):
            acc = first_row + jnp.tile(market_sum[first : first + tile, :], (1, block // lanes))
            for t in range(months):
                spread = gathered[t * scen + first : t * scen + first + tile, :]
                acc = acc + (rows[2 + t : 3 + t, cols] * jnp.exp2(sens_row * spread) - spread)
            staged[idx, first : first + tile, :] = jnp.exp2(acc)
        out_copy(idx).start()

    def turn(t):
        span = pl.ds(pl.multiple_of(t * scen, scen), scen)
        cred_ref[t] = credited_buf[span, :].T[:funds]

    blocks = policies // block
    fetch(0, gathered_even)
    inside = blocks // 2 >= months
    if not inside:
        for t in range(months):
            turn(t)

    @pl.loop(0, blocks // 2)
    def _(pair):
        idx = 2 * pair
        fetch(idx + 1, gathered_odd)
        settle(idx, gathered_even)
        fetch(jnp.minimum(idx + 2, blocks - 1), gathered_even)
        settle(idx + 1, gathered_odd)
        if inside:
            turn(jnp.minimum(pair, months - 1))

    @pl.loop(0, blocks)
    def _(idx):
        out_copy(idx).wait()


def local(
    group,
    count_init,
    value_init,
    durations,
    products,
    policy_fund,
    lapse_base,
    lapse_sens,
    fee_rate,
    fund_share,
    bond_flows,
    bond_fund,
    holdings,
    scen_rates,
):
    funds = fund_share.shape[0]
    months, tenors, scen = scen_rates.shape
    kinds = lapse_base.shape[0]
    policies = count_init.shape[0]
    pol_devs, scen_devs, fund_devs = group
    fund_rows = -(-funds // scen_devs)
    class_rows = -(-(months * kinds) // scen_devs)
    wide = round_up(max(funds, tenors), lanes)
    chunk = -(-(fund_rows + class_rows) // fund_devs)
    vmem = pl.BlockSpec(memory_space=pltpu.VMEM)
    count_row, value_row, dur_row, prod_row, pfund_row, bfund_row, hold_row = (
        x[None, :]
        for x in (
            count_init,
            value_init,
            durations,
            products,
            policy_fund,
            bond_fund,
            holdings,
        )
    )
    few = 24 << 20
    hbm = pl.BlockSpec(memory_space=pltpu.HBM)
    sources = (
        bfund_row,
        hold_row,
        bond_flows.T,
        pfund_row,
        count_row,
        value_row,
        dur_row,
        prod_row,
        lapse_base,
        lapse_sens,
        fee_rate,
        fund_share[None, :],
        scen_rates,
    )
    carried = pl.pallas_call(
        functools.partial(gather_kernel, group, kinds, funds),
        out_shape=(
            jax.ShapeDtypeStruct((scen_devs * (fund_rows + class_rows), wide), f32),
            jax.ShapeDtypeStruct((wide, policies), bf16),
            jax.ShapeDtypeStruct((round_up(2 + months, 8), policies), f32),
            jax.ShapeDtypeStruct((months * scen, 2 * wide), bf16),
            jax.ShapeDtypeStruct((months * scen, wide), f32),
            jax.ShapeDtypeStruct((3 * kinds, wide), f32),
            jax.ShapeDtypeStruct((1, funds), f32),
        ),
        in_specs=[hbm] * len(sources),
        out_specs=(vmem,) * 7,
        scratch_shapes=[
            *(pltpu.VMEM(x.shape, x.dtype) for x in sources[:8]),
            *(pltpu.SMEM(x.shape, x.dtype) for x in sources[8:11]),
            pltpu.VMEM(scen_rates.shape, f32),
            pltpu.SemaphoreType.DMA((len(sources),)),
            pltpu.VMEM((fund_devs, chunk, wide), f32),
            pltpu.VMEM((fund_devs, chunk, wide), f32),
            pltpu.VMEM((pol_devs, chunk, wide), f32),
            pltpu.VMEM((scen_devs * fund_devs, chunk, wide), f32),
            pltpu.SemaphoreType.DMA((2, fund_devs)),
            pltpu.SemaphoreType.DMA((2, pol_devs)),
            pltpu.SemaphoreType.DMA((2, scen_devs * fund_devs)),
        ],
        compiler_params=pltpu.CompilerParams(
            collective_id=0, has_side_effects=True, vmem_limit_bytes=few
        ),
        name="fund_sums",
    )(*(pltpu.with_memory_space_constraint(x, pltpu.HBM) for x in sources))
    block = policies // (2 * max(1, policies // 512))
    return pl.pallas_call(
        functools.partial(project_kernel, scen_devs * fund_rows, kinds, funds, block),
        out_shape=(
            jax.ShapeDtypeStruct((months, funds, scen), f32),
            jax.ShapeDtypeStruct((scen, policies), f32),
        ),
        in_specs=[vmem] * 7,
        out_specs=(vmem, pl.BlockSpec(memory_space=pl.ANY)),
        scratch_shapes=[
            pltpu.VMEM((months * scen, 2 * wide), bf16),
            pltpu.VMEM((months * scen, wide), f32),
            pltpu.VMEM((months * scen, wide), f32),
            pltpu.VMEM((months * scen, block), f32),
            pltpu.VMEM((months * scen, block), f32),
            pltpu.VMEM((scen, lanes), f32),
            pltpu.VMEM((policies // block, scen, block), f32),
            pltpu.SemaphoreType.DMA((policies // block,)),
        ],
        compiler_params=pltpu.CompilerParams(vmem_limit_bytes=few),
        name="project",
    )(*carried)


def solution(mesh):
    in_specs = (
        P(("pol", "fund")),
        P(("pol", "fund")),
        P(("pol", "fund")),
        P(("pol", "fund")),
        P(("pol", "fund")),
        P(),
        P(),
        P(),
        P(),
        P(("pol", "fund"), None),
        P(("pol", "fund")),
        P(("pol", "fund")),
        P(None, None, ("parts", "scen")),
    )
    out_specs = (P(None, None, ("parts", "scen")), P(("parts", "scen"), ("pol", "fund")))
    group = tuple(mesh.shape[name] for name in ("pol", "scen", "fund"))
    return jax.shard_map(
        functools.partial(local, group),
        mesh=mesh,
        in_specs=in_specs,
        out_specs=out_specs,
        check_vma=False,
    )
```
